512 devices in a mesh: head: 8 (over x, core), ctx: 64 (over y, z).
Axes of the slice: x: 4, y: 4, z: 16, core: 2. Of those that a mesh axis runs over, the one named last changes fastest.
Arguments:
- queries: bfloat16 [8, 64, 1024, 128], P('head', 'ctx'), may hold values from -72 to 72
- keys: bfloat16 [8, 262144, 128], P('head', 'ctx'), may hold values from -24 to 24
- values: bfloat16 [8, 262144, 128], P('head', 'ctx'), may hold values from -6 to 6
- kept: int32 [8, 512], P('head'), may hold values from 0 to 262143, as said below
- roots: int32 [8], P('head'), may hold values from 0 to 63
Outputs:
- compact: float32 [8, 512, 128], P('head')
- fit_error: float32 [], replicated
The draws below stay inside these ranges and needn't reach their ends.
Inputs may be any that keep to these rules, and one draw needn't show every extreme that they name: `kept`: per head: 512 distinct increasing positions; at most 32 of them lie within one context device's 4096 positions, and exactly 32 within at least one such device.
All inputs are finite; a program needn't handle non-finite values.
Results may differ from the reference program's by a relative error of at most 0.0003.
Values may be sent and summed in bfloat16 or wider, within the bound.
A program may use at most 64 MiB of HBM per device.

```python
import math
import jax
import jax.numpy as jnp
from jax import lax

HD = 128
R = 1024
SLAB = 4096
KBLK = 1024
M = 512
HEADS = 8
S = 262144
CAP = 32
N_CTX = 64


def kept_positions(base):
    keyring = jax.random.split(jax.random.fold_in(base, 11), 4)
    candidates = N_CTX * CAP
    noise = jax.random.randint(keyring[0], (HEADS, candidates), 0, 4096)
    weight = jax.random.randint(keyring[1], (HEADS, N_CTX), 1, 5)
    busiest = jax.random.randint(keyring[2], (HEADS, 1), 0, N_CTX)
    shard_of = jnp.arange(candidates, dtype=jnp.int32) // CAP
    score = noise * jnp.take(weight, shard_of, axis=1) + jnp.where(shard_of[None, :] == busiest, 65536, 0)
    score = score * candidates + jnp.arange(candidates, dtype=jnp.int32)[None, :]
    chosen = lax.top_k(score, M)[1].astype(jnp.int32)
    shuffles = jax.vmap(lambda subkey: jax.random.permutation(subkey, SLAB)[:CAP])(jax.random.split(keyring[3], HEADS * N_CTX))
    offsets = shuffles.reshape(HEADS, candidates).astype(jnp.int32)
    positions = chosen // CAP * SLAB + jnp.take_along_axis(offsets, chosen, axis=1)
    return jnp.sort(positions, axis=1).astype(jnp.int32)


def make_keys(base):
    raw = jax.random.normal(jax.random.fold_in(base, 23), (HEADS, S, HD), jnp.float32)
    spread = 2.5 * 1.6 ** (jnp.arange(HEADS, dtype=jnp.float32) / max(HEADS - 1, 1))
    result = (jnp.clip(raw, -6.0, 6.0) * spread[:, None, None]).astype(jnp.bfloat16).astype(jnp.float32)
    return result


def draw_keys(key, part):
    return make_keys(key).astype(jnp.bfloat16)


def draw_queries(key, part):
    raw = jax.random.normal(jax.random.fold_in(key, 37), (HEADS, N_CTX, R, HD), jnp.float32)
    result = jnp.clip(raw, -6.0, 6.0)
    return result.astype(jnp.bfloat16)


def draw_kept(key, part):
    return kept_positions(key)


def plant(drawn, own_key, low, top_value):
    longest = drawn.shape.index(max(drawn.shape))
    spots = []
    for shift in (0, 1):
        where = [jax.random.randint(jax.random.fold_in(own_key, axis), (), 0, length) for axis, length in enumerate(drawn.shape)]
        where[longest] = (where[longest] + shift) % drawn.shape[longest]
        spots.append(tuple(where))
    return drawn.at[spots[0]].set(low).at[spots[1]].set(top_value)


def steps_of(own_key, dims, cuts, least, high):
    loudness, own = 1.0, jax.random.fold_in(own_key, 6)
    for position, parts in cuts:
        steps = jnp.exp(jax.random.uniform(jax.random.fold_in(own, position), (parts,), jnp.float32, least / len(cuts), high / len(cuts)))
        loudness = loudness * jnp.repeat(steps, dims[position] // parts).reshape([-1 if axis == position else 1 for axis in range(len(dims))])
    return loudness


def gaussian(own_key, extent, width, most, shards=(), kind=jnp.bfloat16):
    array = width * jax.random.normal(own_key, extent, jnp.float32)
    if shards:
        array = array * steps_of(own_key, extent, shards, -0.22, 0.18)
    return jnp.clip(array, -most, most).astype(kind)


def setup_inputs(seed: int = 0) -> dict:
    streams_of = jax.random.split(jax.random.key(seed), 6)
    return {
        "queries": draw_queries(jax.random.fold_in(streams_of[5], 71), 0),
        "keys": draw_keys(jax.random.fold_in(streams_of[5], 71), 0),
        "values": gaussian(streams_of[2], (HEADS, S, HD), 1.0, 6.0, ((0, 8), (1, 64))),
        "kept": draw_kept(jax.random.fold_in(streams_of[5], 71), 0),
        "roots": plant(jax.random.randint(streams_of[4], (HEADS,), 0, N_CTX), jax.random.fold_in(streams_of[4], 1), 0, N_CTX - 1).astype(jnp.int32),
    }


ridge_share = 0.01

def merge_parts(first, second):
    first_max, first_sum, first_out = first
    second_max, second_sum, second_out = second
    joint = jnp.maximum(first_max, second_max)
    first_scale = jnp.exp(first_max - joint)
    second_scale = jnp.exp(second_max - joint)
    return (joint, first_sum * first_scale + second_sum * second_scale, first_out * first_scale[:, None] + second_out * second_scale[:, None])

def block_partials(queries_ref, key_all, value_all, score_scale):
    blocks = key_all.shape[0] // KBLK
    key_blocks = key_all.reshape(blocks, KBLK, HD)
    value_blocks = value_all.reshape(blocks, KBLK, HD)
    rows = queries_ref.shape[0]

    def visit(carry, pieces):
        key_block, value_block = pieces
        scores = jnp.einsum('rd,kd->rk', queries_ref.astype(jnp.float32), key_block.astype(jnp.float32), preferred_element_type=jnp.float32) * score_scale
        block_max = lax.optimization_barrier(jnp.max(scores, axis=1))
        weights = jnp.exp(scores - block_max[:, None]).astype(jnp.bfloat16)
        block_sum = lax.optimization_barrier(jnp.sum(weights.astype(jnp.float32), axis=1))
        block_out = jnp.dot(weights.astype(jnp.float32), value_block.astype(jnp.float32), preferred_element_type=jnp.float32)
        return (merge_parts(carry, (block_max, block_sum, block_out)), None)
    start = (jnp.full((rows,), -jnp.inf, jnp.float32), jnp.zeros((rows,), jnp.float32), jnp.zeros((rows, HD), jnp.float32))
    return lax.scan(visit, start, (key_blocks, value_blocks))[0]

def compact_softmax(queries_ref, compact_keys, score_scale):
    scores = jnp.einsum('rd,md->rm', queries_ref.astype(jnp.float32), compact_keys.astype(jnp.float32), preferred_element_type=jnp.float32) * score_scale
    return jax.nn.softmax(scores, axis=1)

def inner_left(left, right):
    return lax.dot_general(left.astype(jnp.float32), right.astype(jnp.float32), (((0,), (0,)), ((), ())), precision=lax.Precision.HIGHEST, preferred_element_type=jnp.float32)

def one_head(inputs):
    query_sets, key_all, value_all, kept_rows, root_row = inputs
    score_scale = 1.0 / math.sqrt(HD)
    queries_ref = lax.dynamic_index_in_dim(query_sets, root_row.astype(jnp.int32), 0, keepdims=False)
    run_max, run_sum, run_out = block_partials(queries_ref, key_all, value_all, score_scale)
    target = run_out / run_sum[:, None]
    compact_keys = jnp.take(key_all, kept_rows.astype(jnp.int32), axis=0)
    attend = compact_softmax(queries_ref, compact_keys, score_scale)
    gram = inner_left(attend, attend)
    cross = inner_left(attend, target)
    ridge = ridge_share * jnp.trace(gram) / M
    system = gram + ridge * jnp.eye(M, dtype=jnp.float32)
    factor_low = jnp.linalg.cholesky(system)
    halfway = lax.linalg.triangular_solve(factor_low, cross, left_side=True, lower=True)
    compact = lax.linalg.triangular_solve(factor_low, halfway, left_side=True, lower=True, transpose_a=True)
    fitted = jnp.dot(attend.astype(jnp.float32), compact.astype(jnp.float32), precision=lax.Precision.HIGHEST, preferred_element_type=jnp.float32)
    misfit = fitted - target
    head_error = jnp.sum(misfit * misfit) / jnp.sum(target * target)
    return (compact, head_error)

def reference(queries, keys, values, kept, roots):
    compact, errors = lax.map(one_head, (queries, keys, values, kept, roots))
    return (compact, jnp.mean(errors))
```

```python
import math

import jax
import jax.numpy as jnp
from jax import lax
from jax.experimental import pallas as pl
from jax.experimental.pallas import tpu as pltpu
from jax.sharding import PartitionSpec as P

HD = 128
KBLK = 1024
M = 512
NY = 4
NZ = 16
NHEAD = 8
SLAB = 4096
QC = 256
CC = 128
PAY = QC + CC
NSUB = 3
SUB = PAY // NSUB
BLK = 128
SCALE = 1.0 / math.sqrt(HD)
RIDGE = 0.01
F32 = jnp.float32
BF16 = jnp.bfloat16
HIGHEST = lax.Precision.HIGHEST
MESH = pl.DeviceIdType.MESH


def dotf(a, b, ca, cb, precision=None):
    return lax.dot_general(
        a, b, (((ca,), (cb,)), ((), ())), precision=precision, preferred_element_type=F32
    )


def invert_block(tiles):
    lane = lax.broadcasted_iota(jnp.int32, (8, BLK), 1)
    sub = lax.broadcasted_iota(jnp.int32, (8, BLK), 0)

    def group(_, carry):
        t = list(carry)
        for j in range(8):
            hit = lane == j
            own = sub == j
            pivot = t[0][j : j + 1, j : j + 1]
            inv = 1.0 / jnp.broadcast_to(pivot, (8, BLK))
            row = jnp.broadcast_to(t[0][j : j + 1, :], (8, BLK)) * inv
            row = jnp.where(hit, inv, row)
            cols = [jnp.broadcast_to(x[:, j : j + 1], (8, BLK)) for x in t]
            fresh = [jnp.where(hit, 0.0, x) - c * row for x, c in zip(t, cols)]
            fresh[0] = jnp.where(own, row, fresh[0])
            t = fresh
        t = t[1:] + t[:1]
        return tuple(pltpu.roll(x, BLK - 8, 1) for x in t)

    return lax.fori_loop(0, BLK // 8, group, tuple(tiles))


def sweep_block(s_ref, b):
    lo = b * BLK
    tiles = [s_ref[lo + 8 * i : lo + 8 * i + 8, lo : lo + BLK] for i in range(16)]
    inv = jnp.concatenate(invert_block(tiles), axis=0)
    old = s_ref[lo : lo + BLK, :]
    row = dotf(inv, old, 1, 0, HIGHEST)
    s_ref[lo : lo + BLK, :] = row
    s_ref[lo : lo + BLK, lo : lo + BLK] = inv
    for i in range(M // BLK):
        if i == b:
            continue
        r0 = i * BLK
        col = s_ref[r0 : r0 + BLK, lo : lo + BLK]
        s_ref[r0 : r0 + BLK, lo : lo + BLK] = jnp.zeros((BLK, BLK), F32)
        s_ref[r0 : r0 + BLK, :] -= dotf(col, s_ref[lo : lo + BLK, :], 1, 0, HIGHEST)


def body(
    q_hbm, k_hbm, v_hbm, kept_ref, roots_ref, out_ref, fit_ref,
    q_ref, k_ref, v_ref, vt_ref, pm, rq, fl_own, fl_r, fl_l, qall, cfull,
    osend, orecv, comb, ml_own, rz_o, rz_ml, yown, ybuf, at, s_ref, fit_own, fit_in,
    ld_sem, rq_ss, rq_rs, fr_ss, fr_rs, fl_ss, fl_rs, aq_ss, aq_rs, ac_ss, ac_rs,
    o_ss, o_rs, z_ss, z_rs, m_ss, m_rs, g_ss, g_rs, y_ss, y_rs, h_ss, h_rs,
):
    head = lax.axis_index("head")
    ctx = lax.axis_index("ctx")
    y = ctx // NZ
    z = ctx % NZ

    def at_y(d):
        return (head, ((y + d) % NY) * NZ + z)

    def at_z(t):
        return (head, y * NZ + (z + t) % NZ)

    def at_h(g):
        return ((head + g) % NHEAD, ctx)

    def send(src, dst, ss, rs, dev):
        copy = pltpu.make_async_remote_copy(
            src_ref=src, dst_ref=dst, send_sem=ss, recv_sem=rs, device_id=dev, device_id_type=MESH
        )
        copy.start()
        return copy

    def desc(src, dst, ss, rs):
        return pltpu.make_async_remote_copy(
            src_ref=src, dst_ref=dst, send_sem=ss, recv_sem=rs, device_id=at_z(1), device_id_type=MESH
        )

    ld_q = pltpu.make_async_copy(q_hbm, q_ref, ld_sem.at[0])
    ld_k = pltpu.make_async_copy(k_hbm, k_ref, ld_sem.at[1])
    ld_v = pltpu.make_async_copy(v_hbm, v_ref, ld_sem.at[2])
    ld_q.start()
    ld_k.start()
    ld_v.start()

    barrier = pltpu.get_barrier_semaphore()
    peers = [at_y(1), at_y(2), at_y(3), at_z(1), at_z(NZ - 1)] + [at_h(g) for g in range(1, NHEAD)]
    for dev in peers:
        pl.semaphore_signal(barrier, inc=1, device_id=dev, device_id_type=MESH)

    pending = []

    ld_q.wait()
    mine = jnp.broadcast_to(roots_ref[0], (QC, HD)) == ctx
    for i in range(NY):
        part = q_ref[i * QC : (i + 1) * QC, :].astype(F32)
        pm[i, 0:QC, :] = jnp.where(mine, part, 0.0).astype(BF16)
    pl.semaphore_wait(barrier, len(peers))
    for d in (2, 1, 3):
        to = (y + d) % NY
        pending.append(
            send(pm.at[to, pl.ds(0, QC)], rq.at[d - 1, pl.ds(0, QC)],
                 rq_ss.at[d - 1, 0], rq_rs.at[d - 1, 0], at_y(d))
        )

    ld_k.wait()
    base = (ctx * SLAB).astype(F32)
    kept_t = jnp.transpose(jnp.broadcast_to(kept_ref[...].astype(F32), (BLK, M))) - base
    lane = lax.broadcasted_iota(jnp.int32, (M, BLK), 1).astype(F32)
    s_ref[:, 0:HD] = jnp.zeros((M, HD), F32)

    def pick(c, _):
        first = kept_t - (c * (2 * BLK)).astype(F32)
        a = jnp.where(first == lane, 1.0, 0.0).astype(BF16)
        b = jnp.where(first == lane + float(BLK), 1.0, 0.0).astype(BF16)
        rows = k_ref[pl.ds(pl.multiple_of(c * (2 * BLK), 2 * BLK), 2 * BLK), :]
        s_ref[:, 0:HD] += dotf(jnp.concatenate([a, b], axis=1), rows, 1, 0)
        return 0

    lax.fori_loop(0, SLAB // (2 * BLK), pick, 0)
    for i in range(NY):
        pm[i, QC:PAY, :] = s_ref[i * CC : (i + 1) * CC, 0:HD].astype(BF16)
    for d in (2, 1, 3):
        to = (y + d) % NY
        pending.append(
            send(pm.at[to, pl.ds(QC, CC)], rq.at[d - 1, pl.ds(QC, CC)],
                 rq_ss.at[d - 1, 1], rq_rs.at[d - 1, 1], at_y(d))
        )

    ld_v.wait()
    vt_ref[HD : HD + 16, :] = jnp.ones((16, SLAB), BF16)
    for i in range(SLAB // 512):
        piece = v_ref[i * 512 : (i + 1) * 512, :].astype(F32)
        vt_ref[0:HD, i * 512 : (i + 1) * 512] = jnp.transpose(piece).astype(BF16)

    def gathered(part, lo, size):
        for d in range(1, NY):
            desc(pm.at[0, pl.ds(lo, size)], rq.at[d - 1, pl.ds(lo, size)],
                 rq_ss.at[d - 1, part], rq_rs.at[d - 1, part]).wait_recv()
        total = pm[y, lo : lo + size, :].astype(F32)
        for d in range(1, NY):
            total = total + rq[d - 1, lo : lo + size, :].astype(F32)
        fl_own[lo : lo + size, :] = total.astype(BF16)

    right = at_z(1)
    left = at_z(NZ - 1)
    steps_r, steps_l = NZ // 2, NZ // 2 - 1

    def forward_r(t, u):
        rows = pl.ds(u * SUB, SUB)
        src = fl_own.at[rows] if t == 0 else fl_r.at[t - 1, rows]
        pending.append(send(src, fl_r.at[t, rows], fr_ss.at[t, u], fr_rs.at[t, u], right))

    def forward_l(t, u):
        rows = pl.ds(u * SUB, SUB)
        src = fl_own.at[rows] if t == 0 else fl_l.at[t - 1, rows]
        pending.append(send(src, fl_l.at[t, rows], fl_ss.at[t, u], fl_rs.at[t, u], left))

    gathered(0, 0, QC)
    for u in range(2):
        forward_r(0, u)
        forward_l(0, u)
    gathered(1, QC, CC)
    forward_r(0, 2)
    forward_l(0, 2)
    for t in range(steps_r):
        for u in range(NSUB):
            rows = pl.ds(u * SUB, SUB)
            desc(fl_own.at[rows], fl_r.at[t, rows], fr_ss.at[t, u], fr_rs.at[t, u]).wait_recv()
            if t + 1 < steps_r:
                forward_r(t + 1, u)
            if t < steps_l:
                desc(fl_own.at[rows], fl_l.at[t, rows], fl_ss.at[t, u], fl_rs.at[t, u]).wait_recv()
                if t + 1 < steps_l:
                    forward_l(t + 1, u)

    def summed(lo, size):
        total = fl_own[lo : lo + size, :].astype(F32)
        for t in range(steps_r):
            total = total + fl_r[t, lo : lo + size, :].astype(F32)
        for t in range(steps_l):
            total = total + fl_l[t, lo : lo + size, :].astype(F32)
        return total.astype(BF16)

    qall[0] = summed(0, QC)
    for d in (1, 3, 2):
        pending.append(send(qall.at[0], qall.at[d], aq_ss.at[d - 1], aq_rs.at[d - 1], at_y(NY - d)))
    mine_c = pl.ds(pl.multiple_of(y * CC, CC), CC)
    cfull[mine_c, :] = summed(QC, CC)
    for d in (1, 3, 2):
        pending.append(
            send(cfull.at[mine_c], cfull.at[mine_c], ac_ss.at[d - 1], ac_rs.at[d - 1], at_y(NY - d))
        )

    for d in (0, 1, 3, 2):
        if d:
            desc(qall.at[0], qall.at[d], aq_ss.at[d - 1], aq_rs.at[d - 1]).wait_recv()
        qd = qall[d]
        top, acc = None, None
        for b in range(SLAB // KBLK):
            s = dotf(k_ref[b * KBLK : (b + 1) * KBLK, :], qd, 1, 1)
            high = jnp.max(s, axis=0, keepdims=True) * SCALE
            e = jnp.exp(s * SCALE - high).astype(BF16)
            o = dotf(vt_ref[:, b * KBLK : (b + 1) * KBLK], e, 1, 0)
            if b == 0:
                top, acc = high, o
            else:
                joint = jnp.maximum(top, high)
                acc = acc * jnp.exp(top - joint) + o * jnp.exp(high - joint)
                top = joint
        osend[d, 0 : HD + 8, :] = acc[0 : HD + 8]
        osend[d, HD + 8 : HD + 16, :] = jnp.broadcast_to(top, (8, QC))
        if d:
            pending.append(send(osend.at[d], orecv.at[d - 1], o_ss.at[d - 1], o_rs.at[d - 1], at_y(d)))

    for d in (1, 3, 2):
        desc(cfull.at[mine_c], cfull.at[mine_c], ac_ss.at[d - 1], ac_rs.at[d - 1]).wait_recv()
    for d in range(NY):
        s = dotf(cfull[...], qall[d], 1, 1) * SCALE
        e = jnp.exp(s - jnp.max(s, axis=0, keepdims=True))
        at[d] = e / jnp.sum(e, axis=0, keepdims=True)

    for d in range(1, NY):
        desc(osend.at[d], orecv.at[d - 1], o_ss.at[d - 1], o_rs.at[d - 1]).wait_recv()
    tops = [osend[0, HD + 8 : HD + 9, :]] + [orecv[d, HD + 8 : HD + 9, :] for d in range(NY - 1)]
    joint = jnp.maximum(jnp.maximum(tops[0], tops[1]), jnp.maximum(tops[2], tops[3]))
    total = osend[0, 0 : HD + 8, :] * jnp.exp(tops[0] - joint)
    for d in range(NY - 1):
        total = total + orecv[d, 0 : HD + 8, :] * jnp.exp(tops[d + 1] - joint)
    comb[...] = total[0:HD]
    ml_own[0:1, 0:QC] = total[HD : HD + 1]
    ml_own[0:1, QC : 2 * QC] = joint

    def z_rows(t):
        return pl.ds(pl.multiple_of(((z + t) % NZ) * 8, 8), 8)

    for t in sorted(range(1, NZ), key=lambda t: -min(t, NZ - t)):
        pending.append(send(comb.at[z_rows(t)], rz_o.at[t - 1], z_ss.at[t - 1], z_rs.at[t - 1], at_z(t)))
        pending.append(send(ml_own, rz_ml.at[t - 1], m_ss.at[t - 1], m_rs.at[t - 1], at_z(t)))

    def gram(i, _):
        rows = pl.ds(pl.multiple_of(i * BLK, BLK), BLK)
        total = dotf(at[0, rows, :], at[0], 1, 1, HIGHEST)
        for d in range(1, NY):
            total = total + dotf(at[d, rows, :], at[d], 1, 1, HIGHEST)
        s_ref[rows, :] = total
        return 0

    lax.fori_loop(0, M // BLK, gram, 0)
    eye = lax.broadcasted_iota(jnp.int32, (M, M), 0) == lax.broadcasted_iota(jnp.int32, (M, M), 1)
    trace = jnp.sum(jnp.where(eye, s_ref[...], 0.0), keepdims=True)
    s_ref[...] += jnp.where(eye, trace * (RIDGE / M), 0.0)
    sweep_block(s_ref, 0)

    for t in range(1, NZ):
        desc(comb.at[z_rows(0)], rz_o.at[t - 1], z_ss.at[t - 1], z_rs.at[t - 1]).wait_recv()
        desc(ml_own, rz_ml.at[t - 1], m_ss.at[t - 1], m_rs.at[t - 1]).wait_recv()
    joint = ml_own[0:1, QC : 2 * QC]
    for t in range(NZ - 1):
        joint = jnp.maximum(joint, rz_ml[t, 0:1, QC : 2 * QC])
    w = jnp.exp(ml_own[0:1, QC : 2 * QC] - joint)
    total = comb[z_rows(0), :] * w
    weight = ml_own[0:1, 0:QC] * w
    for t in range(NZ - 1):
        w = jnp.exp(rz_ml[t, 0:1, QC : 2 * QC] - joint)
        total = total + rz_o[t] * w
        weight = weight + rz_ml[t, 0:1, 0:QC] * w
    ybuf[0, z_rows(0), :] = total / weight
    far = sorted(range(1, NZ), key=lambda t: -min(t, NZ - t))
    for t in far:
        pending.append(
            send(ybuf.at[0, z_rows(0)], ybuf.at[0, z_rows(0)], g_ss.at[t - 1], g_rs.at[t - 1], at_z(t))
        )

    def relay(t):
        rows = z_rows(NZ - t)
        for d in range(1, NY):
            pending.append(
                send(ybuf.at[0, rows], ybuf.at[d, rows], y_ss.at[d - 1, t], y_rs.at[d - 1, t], at_y(NY - d))
            )

    relay(0)
    sweep_block(s_ref, 1)
    sweep_block(s_ref, 2)
    for t in reversed(far):
        desc(ybuf.at[0, z_rows(0)], ybuf.at[0, z_rows(NZ - t)], g_ss.at[t - 1], g_rs.at[t - 1]).wait_recv()
        relay(t)
    sweep_block(s_ref, 3)
    for t in range(NZ):
        for d in range(1, NY):
            rows = z_rows(NZ - t)
            desc(ybuf.at[0, rows], ybuf.at[d, rows], y_ss.at[d - 1, t], y_rs.at[d - 1, t]).wait_recv()

    cross = dotf(at[0], ybuf[0], 1, 1, HIGHEST)
    for d in range(1, NY):
        cross = cross + dotf(at[d], ybuf[d], 1, 1, HIGHEST)
    compact = dotf(s_ref[...], cross, 1, 0, HIGHEST)
    out_ref[...] = compact
    misfit = jnp.zeros((1, 1), F32)
    norm = jnp.zeros((1, 1), F32)
    compact_t = jnp.transpose(compact)
    for d in range(NY):
        target = ybuf[d]
        off = dotf(compact_t, at[d], 1, 0, HIGHEST) - target
        misfit = misfit + jnp.sum(off * off, keepdims=True)
        norm = norm + jnp.sum(target * target, keepdims=True)
    fit_own[...] = jnp.broadcast_to(misfit / norm, (8, 128))
    for g in range(1, NHEAD):
        pending.append(send(fit_own, fit_in.at[g - 1], h_ss.at[g - 1], h_rs.at[g - 1], at_h(g)))
    for g in range(1, NHEAD):
        desc(fit_own, fit_in.at[g - 1], h_ss.at[g - 1], h_rs.at[g - 1]).wait_recv()
    total = fit_own[...]
    for g in range(NHEAD - 1):
        total = total + fit_in[g]
    fit_ref[...] = total * (1.0 / NHEAD)
    for copy in pending:
        copy.wait_send()


def per_device(queries, keys, values, kept, roots):
    dma = pltpu.SemaphoreType.DMA
    anywhere = pl.BlockSpec(memory_space=pl.ANY)
    vmem = pl.BlockSpec(memory_space=pltpu.VMEM)
    compact, fit = pl.pallas_call(
        body,
        name="compaction",
        out_shape=(jax.ShapeDtypeStruct((M, HD), F32), jax.ShapeDtypeStruct((8, 128), F32)),
        in_specs=[anywhere, anywhere, anywhere, vmem, pl.BlockSpec(memory_space=pltpu.SMEM)],
        out_specs=(vmem, vmem),
        scratch_shapes=[
            pltpu.VMEM((NY * QC, HD), BF16),
            pltpu.VMEM((SLAB, HD), BF16),
            pltpu.VMEM((SLAB, HD), BF16),
            pltpu.VMEM((HD + 16, SLAB), BF16),
            pltpu.VMEM((NY, PAY, HD), BF16),
            pltpu.VMEM((NY - 1, PAY, HD), BF16),
            pltpu.VMEM((PAY, HD), BF16),
            pltpu.VMEM((NZ // 2, PAY, HD), BF16),
            pltpu.VMEM((NZ // 2 - 1, PAY, HD), BF16),
            pltpu.VMEM((NY, QC, HD), BF16),
            pltpu.VMEM((M, HD), BF16),
            pltpu.VMEM((NY, HD + 16, QC), F32),
            pltpu.VMEM((NY - 1, HD + 16, QC), F32),
            pltpu.VMEM((HD, QC), F32),
            pltpu.VMEM((1, 2 * QC), F32),
            pltpu.VMEM((NZ - 1, 8, QC), F32),
            pltpu.VMEM((NZ - 1, 1, 2 * QC), F32),
            pltpu.VMEM((8, QC), F32),
            pltpu.VMEM((NY, HD, QC), F32),
            pltpu.VMEM((NY, M, QC), F32),
            pltpu.VMEM((M, M), F32),
            pltpu.VMEM((8, 128), F32),
            pltpu.VMEM((NHEAD - 1, 8, 128), F32),
            dma((3,)),
            dma((NY - 1, 2)), dma((NY - 1, 2)),
            dma((NZ // 2, NSUB)), dma((NZ // 2, NSUB)),
            dma((NZ // 2 - 1, NSUB)), dma((NZ // 2 - 1, NSUB)),
            dma((NY - 1,)), dma((NY - 1,)),
            dma((NY - 1,)), dma((NY - 1,)),
            dma((NY - 1,)), dma((NY - 1,)),
            dma((NZ - 1,)), dma((NZ - 1,)),
            dma((NZ - 1,)), dma((NZ - 1,)),
            dma((NZ - 1,)), dma((NZ - 1,)),
            dma((NY - 1, NZ)), dma((NY - 1, NZ)),
            dma((NHEAD - 1,)), dma((NHEAD - 1,)),
        ],
        compiler_params=pltpu.CompilerParams(
            collective_id=0, has_side_effects=True, vmem_limit_bytes=60 * 1024 * 1024
        ),
    )(queries[0, 0], keys[0], values[0], kept, roots)
    return (compact[None], fit[0, 0])


def solution(mesh):
    placed = (
        P("head", "ctx", None, None),
        P("head", "ctx", None),
        P("head", "ctx", None),
        P("head", None),
        P("head"),
    )
    return jax.shard_map(
        per_device,
        mesh=mesh,
        in_specs=placed,
        out_specs=(P("head", None, None), P()),
        check_vma=False,
    )
```
